32 devices in a mesh: rep: 4 (over y, x), shard: 8 (over z, core).
Axes of the slice: x: 2, y: 2, z: 4, core: 2. Of those that a mesh axis runs over, the one named last changes fastest.
Arguments:
- tokens: bfloat16 [4, 1024, 2048], P('rep', 'shard'), may hold values from -6 to 6
- cotangent: bfloat16 [4, 1024, 2048], P('rep', 'shard'), may hold values from -6 to 6
- lengths: int32 [4], P('rep'), may hold values from 256 to 1024, as said below
- adapter_index: int32 [4], P('rep'), may hold values from 0 to 7
- routes: int32 [4, 1024, 8], P('rep', 'shard'), may hold values from 0 to 15, all different within a row; in each aligned block of 128 rows (0 to 127, 128 to 255, ..., all dimensions but the last counted through in order) at most 80 rows name the same one
- attn_norm: bfloat16 [2048], P('shard'), may hold values from 0.5 to 1.5
- mlp_norm: bfloat16 [2048], P('shard'), may hold values from 0.5 to 1.5
- query_norm: bfloat16 [128], P('shard'), may hold values from 0.5 to 1.5
- key_norm: bfloat16 [128], P('shard'), may hold values from 0.5 to 1.5
- w_query: bfloat16 [2048, 4096], P(None, 'shard'), may hold values from -0.125 to 0.125
- key_value_weight: bfloat16 [2, 2048, 512], P(None, 'shard'), may hold values from -0.125 to 0.125
- w_output: bfloat16 [4096, 2048], P('shard'), may hold values from -1.5 to 1.5
- w_router: bfloat16 [2048, 16], P('shard'), may hold values from -0.125 to 0.125
- w_gate: bfloat16 [16, 2048, 768], P(None, 'shard'), may hold values from -0.125 to 0.125
- w_up: bfloat16 [16, 2048, 768], P(None, 'shard'), may hold values from -0.125 to 0.125
- w_down: bfloat16 [16, 2048, 768], P(None, 'shard'), may hold values from -0.625 to 0.625
- attention_down_factor: bfloat16 [8, 3, 2048, 16], P(None, None, 'shard'), may hold values from -0.125 to 0.125
- query_up_factor: bfloat16 [8, 16, 4096], P(None, None, 'shard'), may hold values from -0.5 to 0.5
- key_value_up_factor: bfloat16 [8, 2, 16, 512], P(None, None, None, 'shard'), may hold values from -0.5 to 0.5
- output_down_factor: bfloat16 [8, 4096, 16], P(None, 'shard'), may hold values from -1.5 to 1.5
- output_up_factor: bfloat16 [8, 16, 2048], P(None, None, 'shard'), may hold values from -0.5 to 0.5
- feedforward_down_factor: bfloat16 [8, 3, 2048, 16], P(None, None, 'shard'), may hold values from -0.125 to 0.125
- router_up_factor: bfloat16 [8, 16, 16], P(None, None, 'shard'), may hold values from -0.5 to 0.5
- expert_up_factor: bfloat16 [8, 2, 16, 16, 768], P(None, None, 'shard'), may hold values from -0.5 to 0.5
- down_projection_down_factor: bfloat16 [8, 16, 768, 16], P(None, None, 'shard'), may hold values from -0.625 to 0.625
- down_projection_up_factor: bfloat16 [8, 16, 2048], P(None, None, 'shard'), may hold values from -0.5 to 0.5
Outputs:
- output: bfloat16 [4, 1024, 2048], P('rep', 'shard')
- input_grad: float32 [4, 1024, 2048], P('rep', 'shard')
- attn_squeeze_grad: float32 [8, 3, 2048, 16], P(None, None, 'shard')
- q_expand_grad: float32 [8, 16, 4096], P(None, None, 'shard')
- kv_expand_grad: float32 [8, 2, 16, 512], P(None, None, None, 'shard')
- out_squeeze_grad: float32 [8, 4096, 16], P(None, 'shard')
- out_expand_grad: float32 [8, 16, 2048], P(None, None, 'shard')
- mlp_squeeze_grad: float32 [8, 3, 2048, 16], P(None, None, 'shard')
- router_expand_grad: float32 [8, 16, 16], P(None, None, 'shard')
- expert_expand_grad: float32 [8, 2, 16, 16, 768], P(None, None, 'shard')
- down_squeeze_grad: float32 [8, 16, 768, 16], P(None, None, 'shard')
- down_expand_grad: float32 [8, 16, 2048], P(None, None, 'shard')
The draws below stay inside these ranges and needn't reach their ends.
Inputs may be any that keep to these rules, and one draw needn't show every extreme that they name: `lengths`: at least one sequence has length 1024 and one has 256. `routes`: within the 128 tokens of one device no expert is named by more than 80 of them; in some device one expert is named by exactly 80.
All inputs are finite; a program needn't handle non-finite values.
Results may differ from the reference program's by a relative error of at most 0.025.
Values may be sent and summed in bfloat16 or wider, within the bound.
No kernel may reach another device: no remote copies, remote signals or barrier semaphores. Data moves between devices by JAX's collectives and lax.ppermute only.
A program may use at most 448 MiB of HBM per device.

```python
import math
import jax
import jax.numpy as jnp
import numpy as np
from jax import lax

MODEL_WIDTH = 2048
QUERY_HEADS = 32
KEY_VALUE_HEADS = 4
HEAD_SIZE = 128
FF = 768
EXPERTS = 16
TOP = 8
ADAPTER_RANK = 16
ADAPTER_COUNT = 8
KEY_BLOCK = 512
TOK_DEV = 128
PADDED_LENGTH = 1024
SEQS = 4
CAP = 80


def draw_lengths(key, part):
    key_base, key_top, key_low = jax.random.split(key, 3)
    drawn = jax.random.randint(key_base, (SEQS,), PADDED_LENGTH // 4, PADDED_LENGTH + 1)
    top_slot = jax.random.randint(key_top, (), 0, SEQS)
    low_slot = (top_slot + 1 + jax.random.randint(key_low, (), 0, SEQS - 1)) % SEQS
    slots = jnp.arange(SEQS)
    drawn = jnp.where(slots == top_slot, PADDED_LENGTH, drawn)
    drawn = jnp.where(slots == low_slot, PADDED_LENGTH // 4, drawn)
    return drawn.astype(jnp.int32)


def plant(values, own_key, least, largest):
    longest = values.shape.index(max(values.shape))
    spots = []
    for shift in (0, 1):
        where = [jax.random.randint(jax.random.fold_in(own_key, axis), (), 0, length) for axis, length in enumerate(values.shape)]
        where[longest] = (where[longest] + shift) % values.shape[longest]
        spots.append(tuple(where))
    return values.at[spots[0]].set(least).at[spots[1]].set(largest)


def steps_of(own_key, shape, shards, low, top_value):
    level = 1.0
    for dim, parts in shards:
        steps = jax.random.uniform(jax.random.fold_in(jax.random.fold_in(own_key, 6), dim), (parts,), jnp.float32, low / len(shards), top_value / len(shards))
        level = level * jnp.repeat(jnp.exp(steps), shape[dim] // parts).reshape((-1,) + (1,) * (len(shape) - 1 - dim))
    return level


def assign_block(key, own, number, rows, count, top, most, lean):
    order = jax.random.permutation(key, count)
    crowded, ordinary = shares(count, rows * top, most, lean, True), shares(count, rows * top, most, lean, False)
    places = jnp.arange(count)

    def named(sizes, turn):
        used = int((sizes > 0).sum())
        fixed = max(1, used // 4)
        shifted = fixed + (places - fixed + turn * (used - fixed)) % max(1, count - fixed)
        return jnp.zeros((count,), jnp.int32).at[order[jnp.where(places < fixed, places, shifted)]].set(jnp.asarray(sizes, jnp.int32))

    sizes = jnp.where(number % 4 == 0, named(crowded, number // 4), named(ordinary, number - number // 4 - 1))
    mixed = jax.random.permutation(jax.random.fold_in(own, 3), count)
    donor, sink = mixed[0:count // 2 * 2:2], mixed[1:count // 2 * 2:2]
    slack = jnp.minimum(sizes[donor] - 1, most - sizes[sink]) // 2
    slack = jnp.where((donor == order[0]) | (sink == order[0]) | (sizes[sink] == 0), 0, jnp.maximum(slack, 0))
    shifted = jax.random.randint(jax.random.fold_in(own, 4), (count // 2,), 0, 1 << 20) % (slack + 1)
    sizes = sizes.at[donor].add(-shifted).at[sink].add(shifted)
    members = jnp.searchsorted(jnp.cumsum(sizes), jnp.arange(rows * top), side="right").astype(jnp.int32)
    grid = members.reshape(top, rows).T
    grid = grid[jax.random.permutation(jax.random.fold_in(own, 1), rows)]
    turn = jax.random.randint(jax.random.fold_in(own, 2), (rows, 1), 0, top)
    return jnp.take_along_axis(grid, (jnp.arange(top)[None, :] + turn) % top, axis=1)


def shares(number_of, total, limit, slope, full):
    portions = [(1 << 20) // math.isqrt(rank ** slope) + 1 for rank in range(1, number_of + 1)]
    largest = limit if full else min(limit, max(-(-total // number_of), total * portions[0] // sum(portions)))
    least = 1 if total - largest >= number_of - 1 else 0
    given, surplus = [largest] + [least] * (number_of - 1), total - largest - least * (number_of - 1)
    while surplus > 0:
        candidates = [i for i in range(1, number_of) if given[i] < largest] or [i for i in range(1, number_of) if given[i] < limit]
        mass, left = sum([portions[i] for i in candidates]), surplus
        for i in candidates:
            more = min(limit - given[i], max(1, left * portions[i] // mass), surplus)
            given[i] = given[i] + more
            surplus = surplus - more
    return np.array(given)


def scatter_about(own_key, extent, spread, limit, shards=(), kind=jnp.bfloat16):
    values = spread * jax.random.normal(own_key, extent, jnp.float32)
    if shards:
        values = values * steps_of(own_key, extent, shards, -0.22, 0.18)
    return jnp.clip(values, -limit, limit).astype(kind)


def setup_inputs(seed: int = 0) -> dict:
    streams_of = jax.random.split(jax.random.key(seed), 27)
    tokens = scatter_about(streams_of[0], (SEQS, PADDED_LENGTH, MODEL_WIDTH), 1.0, 6.0, ((0, 4), (1, 8)))
    cotangent = scatter_about(streams_of[1], (SEQS, PADDED_LENGTH, MODEL_WIDTH), 1.0, 6.0, ((0, 4), (1, 8)))
    lengths = draw_lengths(jax.random.fold_in(streams_of[26], 71), 0)
    adapter_index = plant(jax.random.randint(streams_of[3], (SEQS,), 0, ADAPTER_COUNT), jax.random.fold_in(streams_of[3], 1), 0, ADAPTER_COUNT - 1).astype(jnp.int32)
    routes_keys = jax.random.split(jax.random.fold_in(streams_of[4], 1), SEQS * PADDED_LENGTH // TOK_DEV)
    routes_turns = jax.random.permutation(jax.random.fold_in(streams_of[4], 3), SEQS * PADDED_LENGTH // TOK_DEV)
    routes = jax.vmap(lambda own, number: assign_block(jax.random.fold_in(streams_of[4], 2), own, number, TOK_DEV, EXPERTS, TOP, CAP, 1))(routes_keys, routes_turns).reshape((SEQS, PADDED_LENGTH, TOP))
    attn_norm = jnp.clip(1.0 + 0.1 * jax.random.normal(streams_of[5], (MODEL_WIDTH,), jnp.float32), 0.5, 1.5).astype(jnp.bfloat16)
    mlp_norm = jnp.clip(1.0 + 0.1 * jax.random.normal(streams_of[6], (MODEL_WIDTH,), jnp.float32), 0.5, 1.5).astype(jnp.bfloat16)
    query_norm = jnp.clip(1.0 + 0.1 * jax.random.normal(streams_of[7], (HEAD_SIZE,), jnp.float32), 0.5, 1.5).astype(jnp.bfloat16)
    key_norm = jnp.clip(1.0 + 0.1 * jax.random.normal(streams_of[8], (HEAD_SIZE,), jnp.float32), 0.5, 1.5).astype(jnp.bfloat16)
    w_query = scatter_about(streams_of[9], (MODEL_WIDTH, QUERY_HEADS * HEAD_SIZE), MODEL_WIDTH ** -0.5, 0.125, ((1, 8),))
    key_value_weight = scatter_about(streams_of[10], (2, MODEL_WIDTH, KEY_VALUE_HEADS * HEAD_SIZE), MODEL_WIDTH ** -0.5, 0.125, ((1, 8),))
    w_output = scatter_about(streams_of[11], (QUERY_HEADS * HEAD_SIZE, MODEL_WIDTH), (max(QUERY_HEADS * HEAD_SIZE // 256, 1)) ** -0.5, 1.5, ((0, 8),))
    w_router = scatter_about(streams_of[12], (MODEL_WIDTH, EXPERTS), MODEL_WIDTH ** -0.5, 0.125, ((0, 8),))
    w_gate = scatter_about(streams_of[13], (EXPERTS, MODEL_WIDTH, FF), MODEL_WIDTH ** -0.5, 0.125, ((1, 8),))
    w_up = scatter_about(streams_of[14], (EXPERTS, MODEL_WIDTH, FF), MODEL_WIDTH ** -0.5, 0.125, ((1, 8),))
    w_down = scatter_about(streams_of[15], (EXPERTS, MODEL_WIDTH, FF), (FF // 8) ** -0.5, 0.625, ((1, 8),))
    attention_down_factor = scatter_about(streams_of[16], (ADAPTER_COUNT, 3, MODEL_WIDTH, ADAPTER_RANK), MODEL_WIDTH ** -0.5, 0.125, ((2, 8),))
    query_up_factor = scatter_about(streams_of[17], (ADAPTER_COUNT, ADAPTER_RANK, QUERY_HEADS * HEAD_SIZE), 0.08, 0.5, ((2, 8),))
    key_value_up_factor = scatter_about(streams_of[18], (ADAPTER_COUNT, 2, ADAPTER_RANK, KEY_VALUE_HEADS * HEAD_SIZE), 0.08, 0.5, ((3, 8),))
    output_down_factor = scatter_about(streams_of[19], (ADAPTER_COUNT, QUERY_HEADS * HEAD_SIZE, ADAPTER_RANK), (max(QUERY_HEADS * HEAD_SIZE // 256, 1)) ** -0.5, 1.5, ((1, 8),))
    output_up_factor = scatter_about(streams_of[20], (ADAPTER_COUNT, ADAPTER_RANK, MODEL_WIDTH), 0.08, 0.5, ((2, 8),))
    feedforward_down_factor = scatter_about(streams_of[21], (ADAPTER_COUNT, 3, MODEL_WIDTH, ADAPTER_RANK), MODEL_WIDTH ** -0.5, 0.125, ((2, 8),))
    router_up_factor = scatter_about(streams_of[22], (ADAPTER_COUNT, ADAPTER_RANK, EXPERTS), 0.08, 0.5, ((2, 8),))
    expert_up_factor = scatter_about(streams_of[23], (ADAPTER_COUNT, 2, EXPERTS, ADAPTER_RANK, FF), 0.08, 0.5, ((2, 8),))
    down_projection_down_factor = scatter_about(streams_of[24], (ADAPTER_COUNT, EXPERTS, FF, ADAPTER_RANK), (FF // 8) ** -0.5, 0.625, ((2, 8),))
    down_projection_up_factor = scatter_about(streams_of[25], (ADAPTER_COUNT, ADAPTER_RANK, MODEL_WIDTH), 0.08, 0.5, ((2, 8),))
    return dict(tokens=tokens, cotangent=cotangent, lengths=lengths, adapter_index=adapter_index, routes=routes, attn_norm=attn_norm, mlp_norm=mlp_norm, query_norm=query_norm, key_norm=key_norm, w_query=w_query, key_value_weight=key_value_weight, w_output=w_output, w_router=w_router, w_gate=w_gate, w_up=w_up, w_down=w_down, attention_down_factor=attention_down_factor, query_up_factor=query_up_factor, key_value_up_factor=key_value_up_factor, output_down_factor=output_down_factor, output_up_factor=output_up_factor, feedforward_down_factor=feedforward_down_factor, router_up_factor=router_up_factor, expert_up_factor=expert_up_factor, down_projection_down_factor=down_projection_down_factor, down_projection_up_factor=down_projection_up_factor)


EPSILON = 1e-06
THETA_BASE = 1000000.0
ADAPT_SCALE = 2.0
PRECISE = lax.Precision.HIGHEST

@jax.custom_vjp
def reduced_path(v):
    return lax.optimization_barrier(v.astype(jnp.bfloat16)).astype(jnp.float32)

@jax.custom_vjp
def low_back(v):
    return v

def low_keep(v):
    return (reduced_path(v), None)

def low_pass(kept, grad):
    return (grad,)

def back_keep(v):
    return (v, None)

def back_low(kept, grad):
    return (reduced_path(grad),)
reduced_path.defvjp(low_keep, low_pass)
low_back.defvjp(back_keep, back_low)

def full_dot(left, right):
    return jnp.dot(left, right, precision=PRECISE)

def row_norm_apply(vector, gain):
    return vector * lax.rsqrt(lax.optimization_barrier(jnp.mean(vector * vector, axis=-1, keepdims=True)) + EPSILON) * gain

def rotary_apply(vector, cosine_table, sine_table):
    half_n = vector.shape[-1] // 2
    first = vector[..., :half_n]
    second = vector[..., half_n:]
    return jnp.concatenate([first * cosine_table - second * sine_table, second * cosine_table + first * sine_table], axis=-1)

def rope_tables():
    places = jnp.arange(PADDED_LENGTH).astype(jnp.float32)
    inv_freq = THETA_BASE ** (-(jnp.arange(HEAD_SIZE // 2).astype(jnp.float32) * 2.0 / HEAD_SIZE))
    angles = places[:, None] * inv_freq[None, :]
    return (jnp.cos(angles), jnp.sin(angles))

def masked_softmax(scores):
    top_val = lax.optimization_barrier(jnp.max(scores, axis=-1, keepdims=True))
    exp_vals = jnp.exp(scores - top_val)
    return exp_vals / lax.optimization_barrier(jnp.sum(exp_vals, axis=-1, keepdims=True))

def sequence_forward(x_rows, adapter_params, seq_len, routes_seq, frozen):
    g_attn, g_mlp, g_query, gradient_key, query_w, keyval_w, output_w, router_w, gate_all, up_all, down_all, cosine_table, sine_table = frozen
    attn_sq, query_ex, keyval_ex, out_sq, out_ex, mlp_sq, router_ex, expert_ex, down_sq, down_ex = adapter_params
    normed = reduced_path(row_norm_apply(x_rows, g_attn))
    latent = reduced_path(low_back(jnp.einsum('td,cdr->ctr', normed, attn_sq, precision=PRECISE)))
    q_pre = low_back(full_dot(normed, query_w) + ADAPT_SCALE * full_dot(latent[0], query_ex))
    key_value_before = low_back(jnp.einsum('td,cdf->ctf', normed, keyval_w, precision=PRECISE) + ADAPT_SCALE * jnp.einsum('ctr,crf->ctf', latent[1:], keyval_ex, precision=PRECISE))
    query_vectors = reduced_path(rotary_apply(row_norm_apply(q_pre.reshape(PADDED_LENGTH, QUERY_HEADS, HEAD_SIZE), g_query), cosine_table[:, None, :], sine_table[:, None, :]))
    key_vectors = reduced_path(rotary_apply(row_norm_apply(key_value_before[0].reshape(PADDED_LENGTH, KEY_VALUE_HEADS, HEAD_SIZE), gradient_key), cosine_table[:, None, :], sine_table[:, None, :]))
    value_vectors = reduced_path(key_value_before[1].reshape(PADDED_LENGTH, KEY_VALUE_HEADS, HEAD_SIZE))
    group_count = QUERY_HEADS // KEY_VALUE_HEADS
    query_groups = query_vectors.reshape(PADDED_LENGTH, KEY_VALUE_HEADS, group_count, HEAD_SIZE)
    key_pos = jnp.arange(PADDED_LENGTH).astype(jnp.int32)

    def attend(offset):
        q_block = lax.dynamic_slice_in_dim(query_groups, offset, KEY_BLOCK, 0)
        scores = low_back(jnp.einsum('tngd,knd->ngtk', q_block, key_vectors, precision=PRECISE) * HEAD_SIZE ** (-0.5))
        query_pos = offset + jnp.arange(KEY_BLOCK).astype(jnp.int32)
        allowed = (key_pos[None, :] <= query_pos[:, None]) & (key_pos[None, :] < seq_len)
        scores = jnp.where(allowed, scores, -jnp.inf)
        weights = reduced_path(masked_softmax(scores))
        return jnp.einsum('ngtk,knd->tngd', weights, value_vectors, precision=PRECISE)
    starts = (jnp.arange(PADDED_LENGTH // KEY_BLOCK) * KEY_BLOCK).astype(jnp.int32)
    mixed = lax.map(jax.checkpoint(attend), starts)
    attended = reduced_path(low_back(mixed.reshape(PADDED_LENGTH, QUERY_HEADS * HEAD_SIZE)))
    latent_o = reduced_path(low_back(full_dot(attended, out_sq)))
    branch = low_back(full_dot(attended, output_w) + ADAPT_SCALE * full_dot(latent_o, out_ex))
    hidden = x_rows + branch
    mlp_in = reduced_path(row_norm_apply(hidden, g_mlp))
    latent_r = reduced_path(low_back(full_dot(mlp_in, mlp_sq[0])))
    logits = low_back(full_dot(mlp_in, router_w) + ADAPT_SCALE * full_dot(latent_r, router_ex))
    chosen = lax.optimization_barrier(jnp.sum((routes_seq[:, :, None] == jnp.arange(EXPERTS).astype(jnp.int32)[None, None, :]).astype(jnp.float32), axis=1))
    gate_w = masked_softmax(jnp.where(chosen > 0.0, logits, -jnp.inf))

    def expert(running, pieces):
        w_gate_e, w_up_e, w_down_e, expand_g, expand_u, squeeze_d, column = pieces
        expert_in = low_back(mlp_in)
        lat_g = reduced_path(low_back(full_dot(expert_in, mlp_sq[1])))
        lat_u = reduced_path(low_back(full_dot(expert_in, mlp_sq[2])))
        gate_pre = low_back(full_dot(expert_in, w_gate_e) + ADAPT_SCALE * full_dot(lat_g, expand_g))
        up_pre = low_back(full_dot(expert_in, w_up_e) + ADAPT_SCALE * full_dot(lat_u, expand_u))
        activ = reduced_path(gate_pre * jax.nn.sigmoid(gate_pre) * up_pre)
        lat_d = reduced_path(low_back(full_dot(activ, squeeze_d)))
        result = reduced_path(low_back(full_dot(activ, w_down_e.T) + ADAPT_SCALE * full_dot(lat_d, down_ex)))
        return (running + column[:, None] * result, None)
    mixture, _ = lax.scan(jax.checkpoint(expert), jnp.zeros_like(x_rows), (gate_all, up_all, down_all, expert_ex[0], expert_ex[1], down_sq, gate_w.T))
    return hidden + mixture

def reference(tokens, cotangent, lengths, adapter_index, routes, attn_norm, mlp_norm, query_norm, key_norm, w_query, key_value_weight, w_output, w_router, w_gate, w_up, w_down, attention_down_factor, query_up_factor, key_value_up_factor, output_down_factor, output_up_factor, feedforward_down_factor, router_up_factor, expert_up_factor, down_projection_down_factor, down_projection_up_factor):
    cosine_table, sine_table = rope_tables()
    frozen = (attn_norm.astype(jnp.float32), mlp_norm.astype(jnp.float32), query_norm.astype(jnp.float32), key_norm.astype(jnp.float32), w_query.astype(jnp.float32), key_value_weight.astype(jnp.float32), w_output.astype(jnp.float32), w_router.astype(jnp.float32), w_gate.astype(jnp.float32), w_up.astype(jnp.float32), w_down.astype(jnp.float32), cosine_table, sine_table)
    adapter_tables = (attention_down_factor.astype(jnp.float32), query_up_factor.astype(jnp.float32), key_value_up_factor.astype(jnp.float32), output_down_factor.astype(jnp.float32), output_up_factor.astype(jnp.float32), feedforward_down_factor.astype(jnp.float32), router_up_factor.astype(jnp.float32), expert_up_factor.astype(jnp.float32), down_projection_down_factor.astype(jnp.float32), down_projection_up_factor.astype(jnp.float32))

    def per_sequence(summed_grads, pieces):
        x_seq, grad_seq, seq_len, adapter_choice_index, routes_seq = pieces
        adapter_params = tuple((lax.dynamic_index_in_dim(weight_matrix, adapter_choice_index, 0, keepdims=False) for weight_matrix in adapter_tables))

        def forward(x_rows, chosen_adapters):
            return sequence_forward(x_rows, chosen_adapters, seq_len, routes_seq, frozen)
        result, pullback = jax.vjp(forward, x_seq.astype(jnp.float32), adapter_params)
        d_input, d_adapters = pullback(grad_seq.astype(jnp.float32))
        updated = tuple((lax.dynamic_update_index_in_dim(whole, lax.dynamic_index_in_dim(whole, adapter_choice_index, 0, keepdims=False) + part, adapter_choice_index, 0) for whole, part in zip(summed_grads, d_adapters)))
        return (updated, (result.astype(jnp.bfloat16), d_input))
    empty_gradients = tuple((jnp.zeros(weight_matrix.shape, jnp.float32) for weight_matrix in adapter_tables))
    summed_grads, (output, input_grad) = lax.scan(per_sequence, empty_gradients, (tokens, cotangent, lengths, adapter_index, routes))
    return (output, input_grad, summed_grads[0], summed_grads[1], summed_grads[2], summed_grads[3], summed_grads[4], summed_grads[5], summed_grads[6], summed_grads[7], summed_grads[8], summed_grads[9])
```

```python
import jax
import jax.numpy as jnp
from jax import lax
from jax.sharding import PartitionSpec as P

ADAPTER_COUNT = 8
EPSILON = 1e-06
THETA_BASE = 1000000.0
ADAPT_SCALE = 2.0
NEG_FILL = -1e30
EXTRA = 128
BF = jnp.bfloat16
F32 = jnp.float32


def dot(form, left, right):
    return jnp.einsum(form, left, right, preferred_element_type=F32)


def pick_slot(table, index):
    return lax.dynamic_index_in_dim(table, index, 0, keepdims=False)


def row_scale(vector):
    return lax.rsqrt(jnp.mean(vector * vector, axis=-1, keepdims=True) + EPSILON)


def row_norm_back(vector, scale, gain, grad):
    n = vector * scale
    u = grad * gain
    return scale * (u - n * jnp.mean(u * n, axis=-1, keepdims=True))


def rope_rows(count, head_dim):
    places = jnp.arange(count, dtype=jnp.int32).astype(F32)
    inv_freq = THETA_BASE ** (-(jnp.arange(head_dim // 2, dtype=F32) * 2.0 / head_dim))
    angles = places[:, None] * inv_freq[None, :]
    return jnp.cos(angles)[:, None, :], jnp.sin(angles)[:, None, :]


def rotate(vector, cosine, sine):
    half = vector.shape[-1] // 2
    first, second = vector[..., :half], vector[..., half:]
    return jnp.concatenate([first * cosine - second * sine, second * cosine + first * sine], -1)


def to_rows(value, width):
    value = value.reshape(-1, value.shape[-1])
    pieces = [value[:, i : i + width] for i in range(0, value.shape[1], width)]
    return pieces[0] if len(pieces) == 1 else jnp.concatenate(pieces, 0)


def from_rows(rows, lead, columns):
    width = rows.shape[-1]
    height = 1
    for n in lead:
        height *= n
    outer = rows.shape[:-2]
    pieces = [
        rows[..., i * height : (i + 1) * height, :] for i in range(columns // width)
    ]
    value = pieces[0] if len(pieces) == 1 else jnp.concatenate(pieces, -1)
    return value.reshape(outer + tuple(lead) + (columns,))


def fetch_expert_weights(weight, shard_pos, rep_pos, shards, reps):
    experts, rows, ff = weight.shape
    each = experts // shards
    part = rows // reps
    own = lax.dynamic_slice(weight, (each * shard_pos, 0, 0), (each, rows, ff))
    swap = lax.ppermute(
        lax.dynamic_slice(weight, (each * (shard_pos ^ 1), 0, 0), (each, rows, ff)),
        "shard",
        [(i, i ^ 1) for i in range(shards)],
    )
    pieces = []
    for o in range(2, shards):
        block = lax.dynamic_slice(
            weight, (each * (shard_pos ^ o), part * rep_pos, 0), (each, part, ff)
        )
        pieces.append(lax.ppermute(block, "shard", [(i, i ^ o) for i in range(shards)]))
    share = jnp.stack(pieces)
    copies = [share] + [
        lax.ppermute(share, "rep", [(i, i ^ k) for i in range(reps)]) for k in range(1, reps)
    ]
    whole = jnp.zeros((each, shards * rows, ff), weight.dtype)
    whole = lax.dynamic_update_slice(whole, own, (0, shard_pos * rows, 0))
    whole = lax.dynamic_update_slice(whole, swap, (0, (shard_pos ^ 1) * rows, 0))
    for k in range(reps):
        for o in range(2, shards):
            whole = lax.dynamic_update_slice(
                whole,
                copies[k][o - 2],
                (0, (shard_pos ^ o) * rows + (rep_pos ^ k) * part, 0),
            )
    return whole


def per_device(
    tokens,
    cotangent,
    lengths,
    adapter_index,
    routes,
    attn_norm,
    mlp_norm,
    query_norm,
    key_norm,
    w_query,
    key_value_weight,
    w_output,
    w_router,
    w_gate,
    w_up,
    w_down,
    attention_down_factor,
    query_up_factor,
    key_value_up_factor,
    output_down_factor,
    output_up_factor,
    feedforward_down_factor,
    router_up_factor,
    expert_up_factor,
    down_projection_down_factor,
    down_projection_up_factor,
):
    choice = adapter_index[0]
    seq_len = lengths[0]
    shards = lax.axis_size("shard")
    reps = lax.axis_size("rep")
    s = lax.axis_index("shard")
    r = lax.axis_index("rep")
    rows = tokens.shape[1]
    dim = tokens.shape[2]
    total = rows * shards
    dl = attn_norm.shape[0]
    rank = query_up_factor.shape[1]
    head_dim = query_norm.shape[0] * shards
    local_heads = w_query.shape[1] // head_dim
    kv_heads = key_value_weight.shape[2] // head_dim
    sharing = shards // kv_heads
    experts = w_gate.shape[0]
    each = experts // shards
    ff = w_gate.shape[2]
    ff_local = down_projection_down_factor.shape[2]
    kv_cols = key_value_up_factor.shape[3]

    def gather(value, axis=0):
        return lax.all_gather(value, "shard", axis=axis, tiled=True)

    def scatter(value):
        return lax.psum_scatter(value, "shard", scatter_dimension=0, tiled=True)

    x_loc = tokens[0]
    x_all = gather(x_loc)
    route_here = routes[0]
    chosen = jnp.sum(
        (route_here[:, :, None] == jnp.arange(experts, dtype=jnp.int32)).astype(F32), axis=1
    ).astype(BF)
    misc = jnp.concatenate(
        [
            pick_slot(key_value_up_factor, choice).reshape(-1),
            chosen.reshape(-1),
            pick_slot(router_up_factor, choice).T.reshape(-1),
            query_norm,
            key_norm,
        ]
    )
    misc = jnp.pad(misc, (0, -misc.shape[0] % dl)).reshape(-1, dl)
    pack = jnp.concatenate(
        [
            jnp.swapaxes(pick_slot(attention_down_factor, choice), 1, 2).reshape(3 * rank, dl),
            jnp.swapaxes(pick_slot(feedforward_down_factor, choice), 1, 2).reshape(3 * rank, dl),
            pick_slot(output_up_factor, choice),
            pick_slot(down_projection_up_factor, choice),
            w_router.T,
            attn_norm[None],
            mlp_norm[None],
            misc,
        ],
        0,
    )
    pack_all = gather(pack, 1)
    at = 0

    def take(count):
        nonlocal at
        at += count
        return pack_all[at - count : at]

    attn_down = take(3 * rank)
    ff_down = take(3 * rank).reshape(3, rank, dim)
    out_up = take(rank)
    down_up = take(rank)
    router_t = take(experts)
    attn_gain = take(1).astype(F32)
    mlp_gain = take(1).astype(F32)
    misc_all = jnp.swapaxes(pack_all[at:].reshape(-1, shards, dl), 0, 1).reshape(shards, -1)
    at = 0

    def take_misc(count):
        nonlocal at
        at += count
        return misc_all[:, at - count : at]

    kv_up_all = take_misc(2 * rank * kv_cols).reshape(kv_heads, sharing, 2, rank, kv_cols)
    kv_up = jnp.transpose(pick_slot(kv_up_all, s // sharing), (1, 2, 0, 3)).reshape(
        2, rank, head_dim
    )
    chosen_all = take_misc(rows * experts).reshape(total, experts)
    router_up = take_misc(rank * each).reshape(experts, rank)
    query_gain = take_misc(head_dim // shards).reshape(head_dim).astype(F32)
    key_gain = take_misc(head_dim // shards).reshape(head_dim).astype(F32)

    by_head = jnp.transpose(
        key_value_weight.reshape(2, dl, kv_heads, head_dim), (2, 0, 1, 3)
    )
    by_dest = jnp.repeat(by_head, sharing, axis=0)
    kv_weight = jnp.transpose(
        lax.all_to_all(by_dest, "shard", split_axis=0, concat_axis=0, tiled=True), (1, 0, 2, 3)
    ).reshape(2, dim, head_dim)
    down_down = jnp.transpose(pick_slot(down_projection_down_factor, choice), (0, 2, 1)).reshape(
        shards, each * rank, ff_local
    )
    down_down = jnp.transpose(
        lax.all_to_all(down_down, "shard", split_axis=0, concat_axis=0, tiled=True).reshape(
            shards, each, rank, ff_local
        ),
        (1, 2, 0, 3),
    ).reshape(each, rank, ff)
    query_up = pick_slot(query_up_factor, choice)
    out_down = pick_slot(output_down_factor, choice).T
    expert_up = pick_slot(expert_up_factor, choice)
    g_all = gather(cotangent[0])

    with jax.named_scope("fetch_gate"):
        gate_w = fetch_expert_weights(w_gate, s, r, shards, reps)
    with jax.named_scope("fetch_up"):
        up_w = fetch_expert_weights(w_up, s, r, shards, reps)
    with jax.named_scope("fetch_down"):
        down_w = fetch_expert_weights(w_down, s, r, shards, reps)

    cosine, sine = rope_rows(total, head_dim)
    x_all_f = x_all.astype(F32)
    normed = (x_all_f * row_scale(x_all_f) * attn_gain).astype(BF)
    latent = dot("td,rd->tr", normed, attn_down).astype(BF)
    lat_q, lat_k, lat_v = (latent[:, i * rank : (i + 1) * rank] for i in range(3))
    q_pre = dot("td,df->tf", normed, w_query) + ADAPT_SCALE * dot("tr,rf->tf", lat_q, query_up)
    k_pre = dot("td,df->tf", normed, kv_weight[0]) + ADAPT_SCALE * dot(
        "tr,rf->tf", lat_k, kv_up[0]
    )
    v_pre = dot("td,df->tf", normed, kv_weight[1]) + ADAPT_SCALE * dot(
        "tr,rf->tf", lat_v, kv_up[1]
    )
    q_heads = q_pre.reshape(total, local_heads, head_dim)
    k_heads = k_pre.reshape(total, 1, head_dim)
    q_scale = row_scale(q_heads)
    k_scale = row_scale(k_heads)
    query = rotate(q_heads * q_scale * query_gain, cosine, sine).astype(BF)
    key = rotate(k_heads * k_scale * key_gain, cosine, sine)[:, 0].astype(BF)
    value = v_pre.astype(BF)
    place = jnp.arange(total, dtype=jnp.int32)
    allowed = (place[None, :] <= place[:, None]) & (place[None, :] < seq_len)
    factor = head_dim ** (-0.5)
    scores = jnp.where(allowed, dot("tgd,kd->gtk", query, key) * factor, NEG_FILL)
    top = jnp.max(scores, -1, keepdims=True)
    weights = jnp.exp(scores - top)
    norm = jnp.sum(weights, -1, keepdims=True)
    probs = weights / norm
    attended = dot("gtk,kd->tgd", probs.astype(BF), value)
    attended_b = attended.reshape(total, -1).astype(BF)
    lat_o_part = dot("tf,rf->tr", attended_b, out_down).astype(BF)
    branch_part = dot("tf,fd->td", attended_b, w_output) + ADAPT_SCALE * dot(
        "tr,rd->td", lat_o_part, out_up
    )

    def widen(main, extras):
        extra = jnp.concatenate([e.astype(BF) for e in extras], 1)
        extra = jnp.pad(extra, ((0, 0), (0, EXTRA - extra.shape[1])))
        return jnp.concatenate([main.astype(BF), extra], 1)

    summed = scatter(widen(branch_part, [lat_o_part]))
    lat_o_loc = summed[:, dim : dim + rank]
    hidden = x_loc.astype(F32) + summed[:, :dim].astype(F32)
    hidden_scale = row_scale(hidden)
    mlp_loc = (hidden * hidden_scale * mlp_gain).astype(BF)
    mlp_all = gather(mlp_loc)

    lat_ff = dot("td,crd->ctr", mlp_all, ff_down).astype(BF)
    logits = dot("td,ed->te", mlp_all, router_t) + ADAPT_SCALE * dot(
        "tr,er->te", lat_ff[0], router_up
    )
    logits = jnp.where(chosen_all > 0, logits, NEG_FILL)
    gates = jnp.exp(logits - jnp.max(logits, -1, keepdims=True))
    gates = gates * (chosen_all > 0)
    gates = gates / jnp.sum(gates, -1, keepdims=True)
    gates_mine = lax.dynamic_slice_in_dim(gates, s * each, each, 1)
    down_lat = (ADAPT_SCALE * dot("td,rd->tr", g_all, down_up)).astype(BF)
    mixture = 0.0
    d_rows = 0.0
    gate_grads = []
    d_lat_gate = 0.0
    d_lat_up = 0.0
    lat_down_sum = 0.0
    grads_expand = [[], []]
    grads_squeeze = []
    for e in range(each):
        gate = gates_mine[:, e : e + 1]
        back = dot("td,df->tf", g_all, down_w[e]) + dot("tr,rf->tf", down_lat, down_down[e])
        gate_pre = dot("td,df->tf", mlp_all, gate_w[e]) + ADAPT_SCALE * dot(
            "tr,rf->tf", lat_ff[1], expert_up[0, e]
        )
        up_pre = dot("td,df->tf", mlp_all, up_w[e]) + ADAPT_SCALE * dot(
            "tr,rf->tf", lat_ff[2], expert_up[1, e]
        )
        sig = jax.nn.sigmoid(gate_pre)
        silu = gate_pre * sig
        act = silu * up_pre
        act_b = act.astype(BF)
        lat_down = dot("tf,rf->tr", act_b, down_down[e])
        lat_down_sum = lat_down_sum + gate * lat_down
        mixture = mixture + dot("tf,df->td", (gate * act).astype(BF), down_w[e])
        gate_grads.append(gate[:, 0] * jnp.sum(act * back, -1))
        d_act = gate * back
        d_gate = (d_act * up_pre * sig * (1.0 + gate_pre * (1.0 - sig))).astype(BF)
        d_up = (d_act * silu).astype(BF)
        d_rows = d_rows + dot("tf,df->td", d_gate, gate_w[e]) + dot("tf,df->td", d_up, up_w[e])
        d_lat_gate = d_lat_gate + ADAPT_SCALE * dot("tf,rf->tr", d_gate, expert_up[0, e])
        d_lat_up = d_lat_up + ADAPT_SCALE * dot("tf,rf->tr", d_up, expert_up[1, e])
        grads_expand[0].append(ADAPT_SCALE * dot("tr,tf->rf", lat_ff[1], d_gate))
        grads_expand[1].append(ADAPT_SCALE * dot("tr,tf->rf", lat_ff[2], d_up))
        grads_squeeze.append(
            dot("tr,tf->rf", (gate * down_lat.astype(F32)).astype(BF), act_b)
        )
    mixture = mixture + ADAPT_SCALE * dot("tr,rd->td", lat_down_sum.astype(BF), down_up)
    d_rows = (
        d_rows
        + dot("tr,rd->td", d_lat_gate.astype(BF), ff_down[1])
        + dot("tr,rd->td", d_lat_up.astype(BF), ff_down[2])
    )
    mine = (jnp.arange(experts) // each == s).astype(F32)
    gate_grad_cols = jnp.tile(jnp.stack(gate_grads, 1), (1, shards)) * mine
    summed = scatter(widen(d_rows, [gate_grad_cols, d_lat_gate, d_lat_up, lat_down_sum]))
    gate_grad = summed[:, dim : dim + experts].astype(F32)
    extras = summed[:, dim + experts : dim + experts + 3 * rank]
    gates_loc = lax.dynamic_slice_in_dim(gates, s * rows, rows, 0)
    d_logits = (gate_grad - gates_loc * jnp.sum(gate_grad, -1, keepdims=True)).astype(BF)
    d_lat_r = (ADAPT_SCALE * dot("te,er->tr", d_logits, router_up)).astype(BF)
    d_mlp = (
        summed[:, :dim].astype(F32)
        + dot("te,ed->td", d_logits, router_t)
        + dot("tr,rd->td", d_lat_r, ff_down[0])
    )
    d_hidden = cotangent[0].astype(F32) + row_norm_back(hidden, hidden_scale, mlp_gain, d_mlp)
    wide = gather(widen(d_hidden, [d_logits, extras, lat_o_loc, d_lat_r]))
    mix_loc = scatter(mixture.astype(BF))
    output = (hidden + mix_loc.astype(F32)).astype(BF)[None]

    d_branch = wide[:, :dim]
    at = dim

    def take_wide(count):
        nonlocal at
        at += count
        return wide[:, at - count : at]

    d_logits_all = take_wide(experts)
    d_lat_gate_all = take_wide(rank)
    d_lat_up_all = take_wide(rank)
    lat_down_all = take_wide(rank)
    lat_o_all = take_wide(rank)
    d_lat_r_all = take_wide(rank)
    d_lat_o = (ADAPT_SCALE * dot("td,rd->tr", d_branch, out_up)).astype(BF)
    d_attended = (
        dot("td,fd->tf", d_branch, w_output) + dot("tr,rf->tf", d_lat_o, out_down)
    ).astype(BF)
    d_heads = d_attended.reshape(total, local_heads, head_dim)
    delta = jnp.sum(d_heads.astype(F32) * attended, -1).T[:, :, None]
    d_prob = dot("tgd,kd->gtk", d_heads, value)
    d_score = (probs * (d_prob - delta)).astype(BF)
    d_value = dot("gtk,tgd->kd", probs.astype(BF), d_heads)
    d_query = dot("gtk,kd->tgd", d_score, key) * factor
    d_key = dot("gtk,tgd->kd", d_score, query)[:, None] * factor
    d_q_pre = row_norm_back(q_heads, q_scale, query_gain, rotate(d_query, cosine, -sine))
    d_k_pre = row_norm_back(k_heads, k_scale, key_gain, rotate(d_key, cosine, -sine))
    d_q_pre = d_q_pre.reshape(total, -1).astype(BF)
    d_k_pre = d_k_pre[:, 0].astype(BF)
    d_v_pre = d_value.astype(BF)
    d_latent = jnp.concatenate(
        [
            ADAPT_SCALE * dot("tf,rf->tr", d_q_pre, query_up),
            ADAPT_SCALE * dot("tf,rf->tr", d_k_pre, kv_up[0]),
            ADAPT_SCALE * dot("tf,rf->tr", d_v_pre, kv_up[1]),
        ],
        1,
    ).astype(BF)
    d_normed = (
        dot("tf,df->td", d_q_pre, w_query)
        + dot("tf,df->td", d_k_pre, kv_weight[0])
        + dot("tf,df->td", d_v_pre, kv_weight[1])
        + dot("tr,rd->td", d_latent, attn_down)
    )
    d_normed_loc = scatter(d_normed.astype(BF)).astype(F32)
    x_loc_f = x_loc.astype(F32)
    input_grad = (
        d_hidden + row_norm_back(x_loc_f, row_scale(x_loc_f), attn_gain, d_normed_loc)
    )[None]

    def mine_cols(value):
        return lax.dynamic_slice_in_dim(value, s * dl, dl, 1)

    grad_q_up = ADAPT_SCALE * dot("tr,tf->rf", lat_q, d_q_pre)
    grad_out_down = dot("tr,tf->rf", d_lat_o, attended_b)
    grad_out_up = ADAPT_SCALE * dot("tr,td->rd", lat_o_all, mine_cols(d_branch))
    d_lat_ff = jnp.concatenate([d_lat_r_all, d_lat_gate_all, d_lat_up_all], 1)
    grad_ff_down = dot("tr,td->rd", d_lat_ff, mine_cols(mlp_all))
    grad_down_up = ADAPT_SCALE * dot("tr,td->rd", lat_down_all, mine_cols(g_all))
    grad_router = ADAPT_SCALE * dot(
        "te,tr->er", lax.dynamic_slice_in_dim(d_logits_all, s * each, each, 1), lat_ff[0]
    )
    grad_expert = jnp.stack([jnp.stack(grads_expand[0]), jnp.stack(grads_expand[1])])
    router_rows = jnp.pad(
        jnp.concatenate(
            [grad_router.reshape(-1), jnp.full((1,), choice.astype(F32))]
        ),
        (0, dl - each * rank - 1),
    ).reshape(1, dl)
    whole_pieces = [
        to_rows(grad_q_up, dl),
        to_rows(grad_out_down, dl),
        grad_out_up,
        grad_ff_down,
        grad_down_up,
        router_rows,
        to_rows(grad_expert, dl),
    ]
    sizes = [p.shape[0] for p in whole_pieces]
    shared = lax.all_gather(jnp.concatenate(whole_pieces, 0).astype(BF), "rep", axis=0)
    shared = shared.astype(F32)
    at = 0
    split = []
    for n in sizes:
        split.append(shared[:, at : at + n])
        at += n

    grad_attn_down = dot("tr,td->rd", d_latent, normed)
    to_dest = jnp.transpose(grad_attn_down.reshape(3 * rank, shards, dl), (1, 0, 2))
    grad_kv_up = ADAPT_SCALE * jnp.stack(
        [dot("tr,tf->rf", lat_k, d_k_pre), dot("tr,tf->rf", lat_v, d_v_pre)]
    )
    kv_dest = jnp.transpose(
        grad_kv_up.reshape(2, rank, sharing, kv_cols), (2, 0, 1, 3)
    ).reshape(sharing, -1)
    kv_dest = jnp.tile(kv_dest, (kv_heads, 1)) * (
        jnp.arange(shards) // sharing == s // sharing
    ).astype(F32)[:, None]
    kv_dest = kv_dest.reshape(shards, -1, dl)
    down_dest = jnp.transpose(
        jnp.stack(grads_squeeze).reshape(each, rank, shards, ff_local), (2, 0, 1, 3)
    ).reshape(shards, -1, dl)
    sent = jnp.concatenate([to_dest, kv_dest, down_dest], 1).astype(BF)
    n_rows = sent.shape[1]
    sent = jnp.broadcast_to(sent[None], (reps,) + sent.shape).reshape(reps * shards, n_rows, dl)
    got = lax.all_to_all(sent, ("rep", "shard"), split_axis=0, concat_axis=0, tiled=True)
    got = got.reshape(reps, shards, n_rows, dl).astype(F32)
    n_attn = 3 * rank
    n_kv = kv_dest.shape[1]
    got_attn = jnp.sum(got[:, :, :n_attn], 1)
    got_kv = jnp.sum(got[:, :, n_attn : n_attn + n_kv], 1)
    got_down = got[:, :, n_attn + n_kv :].reshape(reps, experts, rank, ff_local)

    owners = split[5][:, 0, each * rank].astype(jnp.int32)
    slots = (jnp.arange(ADAPTER_COUNT, dtype=jnp.int32)[:, None] == owners[None, :]).astype(F32)

    def place_slots(pieces):
        hot = slots.reshape(slots.shape + (1,) * (pieces.ndim - 1))
        out = 0.0
        for i in range(reps):
            out = out + hot[:, i] * pieces[i][None]
        return out

    def turned(value):
        return jnp.swapaxes(value, -1, -2)

    cols = local_heads * head_dim
    return (
        output,
        input_grad,
        turned(place_slots(got_attn.reshape(reps, 3, rank, dl))),
        place_slots(from_rows(split[0], (rank,), cols)),
        place_slots(got_kv.reshape(reps, 2, rank, kv_cols)),
        turned(place_slots(from_rows(split[1], (rank,), cols))),
        place_slots(split[2]),
        turned(place_slots(split[3].reshape(reps, 3, rank, dl))),
        turned(place_slots(split[5][:, 0, : each * rank].reshape(reps, each, rank))),
        place_slots(from_rows(split[6], (2, each, rank), ff)),
        turned(place_slots(got_down)),
        place_slots(split[4]),
    )


def solution(mesh):
    in_specs = (
        P("rep", "shard", None),
        P("rep", "shard", None),
        P("rep"),
        P("rep"),
        P("rep", "shard", None),
        P("shard"),
        P("shard"),
        P("shard"),
        P("shard"),
        P(None, "shard"),
        P(None, "shard", None),
        P("shard", None),
        P("shard", None),
        P(None, "shard", None),
        P(None, "shard", None),
        P(None, "shard", None),
        P(None, None, "shard", None),
        P(None, None, "shard"),
        P(None, None, None, "shard"),
        P(None, "shard", None),
        P(None, None, "shard"),
        P(None, None, "shard", None),
        P(None, None, "shard"),
        P(None, None, "shard", None, None),
        P(None, None, "shard", None),
        P(None, None, "shard"),
    )
    out_specs = (
        P("rep", "shard", None),
        P("rep", "shard", None),
        P(None, None, "shard", None),
        P(None, None, "shard"),
        P(None, None, None, "shard"),
        P(None, "shard", None),
        P(None, None, "shard"),
        P(None, None, "shard", None),
        P(None, None, "shard"),
        P(None, None, "shard", None, None),
        P(None, None, "shard", None),
        P(None, None, "shard"),
    )
    return jax.shard_map(
        per_device, mesh=mesh, in_specs=in_specs, out_specs=out_specs, check_vma=False
    )
```
